32 devices in a mesh: dp: 8 (over y, x, core), tensor: 4 (over z).
Axes of the slice: x: 2, y: 2, z: 4, core: 2. Of those that a mesh axis runs over, the one named last changes fastest.
Arguments:
- activations: bfloat16 [8192, 28672], P('dp', 'tensor'), may hold values from -6 to 6
- out_grads: bfloat16 [8192, 8192], P('dp', 'tensor'), may hold values from -6 to 6
- proj_in: bfloat16 [28672, 64], P('tensor'), may hold values from -0.03125 to 0.03125
- proj_out: bfloat16 [8192, 64], P('tensor'), may hold values from -0.0625 to 0.0625
- validation: bfloat16 [512, 4096], P('tensor', 'dp'), may hold values from -0.09375 to 0.09375
- doc_lengths: int32 [8, 32], P('dp'), may hold values from 0 to 1024, as said below
- owner_rows: int32 [8, 32], P('dp'), may hold values from 0 to 255, as said below
Outputs:
- scores: bfloat16 [256, 512], P('dp', 'tensor')
The draws below stay inside these ranges and needn't reach their ends.
Inputs may be any that keep to these rules, and one draw needn't show every extreme that they name: `doc_lengths`: in each row the first 1 to 32 entries are positive and sum to 1024, the rest are zero; some row has 32 documents and some row a single document. `owner_rows`: A permutation of 0 to 256 - 1 over all entries; with owner = row // 32, the slots of one row go to 8 distinct owners, exactly 4 slot to each.
All inputs are finite; a program needn't handle non-finite values.
Results may differ from the reference program's by a relative error of at most 0.0098.
Values may be sent and summed in bfloat16 or wider, within the bound.
No kernel may reach another device: no remote copies, remote signals or barrier semaphores. Data moves between devices by JAX's collectives and lax.ppermute only.
A program may use at most 64 MiB of HBM per device.

```python
import jax
import jax.numpy as jnp
from jax import lax

D = 8192
FF = 28672
K = 64
NVAL = 512
TOK_DEV = 1024
MAXDOC = 32
SLOTS = 4
SK = 4096
TOKENS = 8192
N_DP = 8


def draw_doc_lengths(key, part):
    first_key, second_key, third_key = jax.random.split(key, 3)
    counts = jax.random.randint(first_key, (N_DP,), MAXDOC // 2, MAXDOC + 1)
    chosen = jax.random.randint(second_key, (), 0, N_DP)
    rows_index = jnp.arange(N_DP)
    counts = jnp.where(rows_index == chosen, MAXDOC, counts)
    counts = jnp.where(rows_index == (chosen + 1) % N_DP, 1, counts)
    cut_points = jax.vmap(lambda row_key: jax.random.permutation(row_key, TOK_DEV - 1))(jax.random.split(third_key, N_DP)) + 1
    cut_points = cut_points[:, :MAXDOC - 1]
    indices = jnp.arange(MAXDOC - 1)
    cut_points = jnp.where(indices[None, :] < counts[:, None] - 1, cut_points, TOK_DEV)
    sorted_cuts = jnp.sort(cut_points, axis=1)
    boundaries = jnp.concatenate([jnp.zeros((N_DP, 1), jnp.int32), sorted_cuts.astype(jnp.int32), jnp.full((N_DP, 1), TOK_DEV, jnp.int32)], axis=1)
    return (boundaries[:, 1:] - boundaries[:, :-1]).astype(jnp.int32)


def draw_owner_rows(key, part):
    shift_key, slot_key = jax.random.split(jax.random.fold_in(key, 7), 2)
    groups = MAXDOC // SLOTS
    offsets = jax.random.permutation(shift_key, N_DP)[:groups]
    shifts = jax.random.permutation(jax.random.fold_in(shift_key, 1), jnp.repeat(offsets, SLOTS))
    source_perm = jax.random.permutation(jax.random.fold_in(shift_key, 2), N_DP)
    owner_perm = jax.random.permutation(jax.random.fold_in(shift_key, 3), N_DP)
    positions = (source_perm[:, None] + shifts[None, :]) % N_DP
    owners = owner_perm[positions]
    slot_perm = jax.vmap(lambda row_key: jax.random.permutation(row_key, MAXDOC))(jax.random.split(slot_key, N_DP))
    columns = jnp.arange(MAXDOC)
    slots = slot_perm[owners, columns[None, :]]
    return (owners * MAXDOC + slots).astype(jnp.int32)


def steps_of(stream_key, shape, cuts, smallest, largest):
    loudness, own = 1.0, jax.random.fold_in(stream_key, 6)
    for axis_at, parts in cuts:
        heights = jnp.exp(jax.random.uniform(jax.random.fold_in(own, axis_at), (parts,), jnp.float32, smallest / len(cuts), largest / len(cuts)))
        loudness = loudness * jnp.repeat(heights, shape[axis_at] // parts).reshape([-1 if axis == axis_at else 1 for axis in range(len(shape))])
    return loudness


def centred(own_key, dims, deviation, most, cuts=(), kind=jnp.bfloat16):
    loudness = steps_of(own_key, dims, cuts, -0.22, 0.18) if cuts else 1.0
    values = jax.random.normal(own_key, dims, jnp.float32) * deviation * loudness
    return jnp.minimum(jnp.maximum(values, -most), most).astype(kind)


def setup_inputs(seed: int = 0) -> dict:
    key_of = jax.random.split(jax.random.key(seed), 8)
    activations = centred(key_of[0], (TOKENS, FF), 1.0, 6.0, ((0, 8), (1, 4)))
    out_grads = centred(key_of[1], (TOKENS, D), 1.0, 6.0, ((0, 8), (1, 4)))
    proj_in = centred(key_of[2], (FF, K), FF ** -0.5, 0.03125, ((0, 4),))
    proj_out = centred(key_of[3], (D, K), D ** -0.5, 0.0625, ((0, 4),))
    validation = centred(key_of[4], (NVAL, SK), SK ** -0.5, 0.09375, ((0, 4), (1, 8)))
    doc_lengths = draw_doc_lengths(jax.random.fold_in(key_of[7], 71), 0)
    owner_rows = draw_owner_rows(jax.random.fold_in(key_of[7], 71), 0)
    return {"activations": activations, "out_grads": out_grads, "proj_in": proj_in, "proj_out": proj_out, "validation": validation, "doc_lengths": doc_lengths, "owner_rows": owner_rows}


def row_sketch(act_row, grad_row, lengths, proj_in, proj_out):
    act_proj = jnp.dot(act_row, proj_in, preferred_element_type=jnp.float32)
    grad_proj = jnp.dot(grad_row, proj_out, preferred_element_type=jnp.float32)
    tokens = act_proj.shape[0]
    outer_prod = (act_proj[:, :, None] * grad_proj[:, None, :]).reshape(tokens, -1)
    starts = (jnp.cumsum(lengths) - lengths).astype(jnp.int32)
    positions = jnp.arange(tokens, dtype=jnp.int32)
    member = ((positions[None, :] >= starts[:, None]) & (positions[None, :] < starts[:, None] + lengths[:, None])).astype(jnp.float32)
    summed = jnp.dot(member, outer_prod, precision=lax.Precision.HIGHEST, preferred_element_type=jnp.float32)
    scaling = 1.0 / jnp.sqrt(jnp.maximum(lengths, 1).astype(jnp.float32))
    return (summed * scaling[:, None]).astype(jnp.bfloat16)

def reference(activations, out_grads, proj_in, proj_out, validation, doc_lengths, owner_rows):
    act_rows = activations.reshape(N_DP, TOK_DEV, FF)
    grad_rows = out_grads.reshape(N_DP, TOK_DEV, D)
    sketches = lax.map(lambda items: row_sketch(items[0], items[1], items[2], proj_in, proj_out), (act_rows, grad_rows, doc_lengths))
    flat = sketches.reshape(N_DP * MAXDOC, K * K)
    local = jnp.dot(flat, validation.T, preferred_element_type=jnp.float32).astype(jnp.bfloat16)
    is_live = doc_lengths.reshape(-1) > 0
    local = jnp.where(is_live[:, None], local, jnp.zeros_like(local))
    result = jnp.zeros((N_DP * MAXDOC, NVAL), jnp.bfloat16)
    return result.at[owner_rows.reshape(-1)].set(local)
```

```python
import functools

import jax
import jax.numpy as jnp
from jax import lax
from jax.experimental import pallas as pl
from jax.experimental.pallas import tpu as pltpu
from jax.sharding import PartitionSpec as P

BF16, F32 = jnp.bfloat16, jnp.float32
NT = (((1,), (1,)), ((), ()))
VMEM_LIMIT = 48 << 20


def swap(x, axis, k):
    return lax.ppermute(x, axis, [(i, i ^ k) for i in range(lax.axis_size(axis))])


def project_kernel(steps, chunk_ref, act_ref, grad_ref, wa_ref, wg_ref, out_ref, acc_a, acc_g):
    step = pl.program_id(0)

    @pl.when(step == 0)
    def _():
        acc_a[...] = jnp.zeros_like(acc_a)
        acc_g[...] = jnp.zeros_like(acc_g)

    ka, kg = act_ref.shape[1], grad_ref.shape[1]
    wa = wa_ref[:, pl.ds(pl.multiple_of(step * ka, 128), ka)]
    wg = wg_ref[:, pl.ds(pl.multiple_of(step * kg, 128), kg)]
    acc_a[...] += lax.dot_general(act_ref[...], wa, NT, preferred_element_type=F32)
    acc_g[...] += lax.dot_general(grad_ref[...], wg, NT, preferred_element_type=F32)

    @pl.when(step == steps - 1)
    def _():
        out_ref[...] = jnp.concatenate([acc_a[...], acc_g[...]], axis=1).astype(out_ref.dtype)


def project(chunk, activations, out_grads, wa, wg, rows, steps, name):
    ff, d = activations.shape[1], out_grads.shape[1]
    k = wa.shape[0]
    return pl.pallas_call(
        functools.partial(project_kernel, steps),
        out_shape=jax.ShapeDtypeStruct((rows, 2 * k), BF16),
        grid_spec=pltpu.PrefetchScalarGridSpec(
            num_scalar_prefetch=1,
            grid=(steps,),
            in_specs=[
                pl.BlockSpec((rows, ff // steps), lambda i, c: (c[0], i)),
                pl.BlockSpec((rows, d // steps), lambda i, c: (c[0], i)),
                pl.BlockSpec(memory_space=pltpu.VMEM),
                pl.BlockSpec(memory_space=pltpu.VMEM),
            ],
            out_specs=pl.BlockSpec((rows, 2 * k), lambda i, c: (0, 0)),
            scratch_shapes=[pltpu.VMEM((rows, k), F32), pltpu.VMEM((rows, k), F32)],
        ),
        compiler_params=pltpu.CompilerParams(vmem_limit_bytes=VMEM_LIMIT),
        cost_estimate=pl.CostEstimate(
            flops=2 * rows * (ff + d) * k, bytes_accessed=2 * rows * (ff + d), transcendentals=0
        ),
        name=name,
    )(chunk, activations, out_grads, wa, wg)


def score_kernel(n_chunks, n_blocks, group, place_ref, bounds_ref, scale_ref, select_ref, labels_ref, *refs):
    chunks, blocks = refs[:n_chunks], refs[n_chunks : n_chunks + n_blocks]
    out_ref, left, right, member, sketch = refs[n_chunks + n_blocks :]
    rows, k = chunks[0].shape[0], chunks[0].shape[1] // 2
    docs = bounds_ref.shape[1]
    for c, ref in enumerate(chunks):
        turned = ref[...].astype(F32).T.astype(BF16)
        left[:, c * rows : (c + 1) * rows] = turned[:k].astype(F32)
        right[:, c * rows : (c + 1) * rows] = turned[k:]
        at = place_ref[c] * rows + lax.broadcasted_iota(jnp.int32, (rows, docs), 0)
        inside = (at >= bounds_ref[0:1, :]) & (at < bounds_ref[1:2, :])
        member[c * rows : (c + 1) * rows, :] = inside.astype(F32).astype(BF16)
    grads = right[...]
    for i in range(0, k, group):
        outer = jnp.concatenate(
            [left[j : j + 1, :].astype(BF16) * grads for j in range(i, i + group)], axis=0
        )
        summed = jnp.dot(outer, member[...], preferred_element_type=F32)
        sketch[i * k : (i + group) * k, :] = (summed * scale_ref[...]).astype(BF16)
    wide = blocks[0].shape[1]
    local = jnp.zeros((blocks[0].shape[0], docs), F32)
    for b, ref in enumerate(blocks):
        start = pl.multiple_of(place_ref[n_chunks + b] * wide, wide)
        local += jnp.dot(ref[...], sketch[pl.ds(start, wide), :], preferred_element_type=F32)
    packed = lax.dot_general(select_ref[...], local.astype(BF16), NT, preferred_element_type=F32)
    out_ref[...] = (packed + labels_ref[...]).astype(BF16)


def score(place, bounds, scaling, select, labels, chunks, blocks):
    tokens = len(chunks) * chunks[0].shape[0]
    k = chunks[0].shape[1] // 2
    docs = bounds.shape[1]
    group = 8
    vmem = pl.BlockSpec(memory_space=pltpu.VMEM)
    nval = blocks[0].shape[0]
    return pl.pallas_call(
        functools.partial(score_kernel, len(chunks), len(blocks), group),
        out_shape=jax.ShapeDtypeStruct((select.shape[0], nval), BF16),
        in_specs=[pl.BlockSpec(memory_space=pltpu.SMEM)] + [vmem] * (4 + len(chunks) + len(blocks)),
        out_specs=vmem,
        scratch_shapes=[
            pltpu.VMEM((k, tokens), F32),
            pltpu.VMEM((k, tokens), BF16),
            pltpu.VMEM((tokens, docs), BF16),
            pltpu.VMEM((k * k, docs), BF16),
        ],
        compiler_params=pltpu.CompilerParams(vmem_limit_bytes=VMEM_LIMIT),
        cost_estimate=pl.CostEstimate(
            flops=2 * k * k * docs * (tokens + nval), bytes_accessed=2 * k * k * nval, transcendentals=0
        ),
        name="score",
    )(place, bounds, scaling, select, labels, *chunks, *blocks)


def shards(activations, out_grads, proj_in, proj_out, validation, doc_lengths, owner_rows):
    devices, parts = lax.axis_size("dp"), lax.axis_size("tensor")
    me, part = lax.axis_index("dp"), lax.axis_index("tensor")
    tokens, maxdoc = activations.shape[0], doc_lengths.shape[1]
    rows = tokens // parts

    half = [validation] + [swap(validation, "dp", b) for b in range(2, devices, 2)]
    other = swap(jnp.concatenate(half, axis=0), "dp", 1)
    nval = validation.shape[0]
    blocks = []
    for b in range(devices // 2):
        blocks += [half[b], other[b * nval : (b + 1) * nval]]

    wa, wg = proj_in.T, proj_out.T
    got, own = [], None
    for peer in list(range(parts - 1, 0, -1)) + [0]:
        partial = project(
            jnp.array([0], jnp.int32) + (part ^ peer), activations, out_grads, wa, wg, rows, 4, f"project{peer}"
        )
        if peer:
            got.append(swap(partial, "tensor", peer))
        else:
            own = partial
    total = own.astype(F32)
    for piece in got:
        total = total + piece.astype(F32)
    mine = total.astype(BF16)
    chunks = [mine] + [swap(mine, "tensor", peer) for peer in range(1, parts)]

    lengths, out_rows = doc_lengths[0], owner_rows[0]
    indices = jnp.arange(maxdoc, dtype=jnp.int32)
    starts = jnp.sum(jnp.where(indices[:, None] < indices[None, :], lengths[:, None], 0), axis=0)
    bounds = jnp.stack([starts, starts + lengths])
    scaling = (1.0 / jnp.sqrt(jnp.maximum(lengths, 1).astype(F32)))[None, :]

    per_owner = max(1, maxdoc // devices)
    height = -(-2 * per_owner // 8) * 8
    owners, out_slot = out_rows // maxdoc, out_rows % maxdoc
    earlier = (owners[None, :] == owners[:, None]) & (indices[None, :] < indices[:, None])
    target = owners * height + jnp.sum(earlier.astype(jnp.int32), axis=1)
    at = jnp.arange(devices * height, dtype=jnp.int32)
    select = (target[None, :] == at[:, None]).astype(BF16)
    label = jnp.where(lengths > 0, out_slot, -1)
    labels = jnp.sum(jnp.where(target[None, :] + per_owner == at[:, None], label[None, :], 0), axis=1)
    labels = jnp.broadcast_to(labels.astype(F32)[:, None], (devices * height, nval))

    place = jnp.concatenate(
        [part ^ jnp.arange(parts, dtype=jnp.int32), me ^ jnp.arange(devices, dtype=jnp.int32)]
    )
    payload = score(place, bounds, scaling, select, labels, chunks, blocks)
    got_rows = lax.all_to_all(
        payload.reshape(devices, height, nval), "dp", split_axis=0, concat_axis=0, tiled=True
    )
    data = got_rows[:, :per_owner].reshape(devices * per_owner, nval)
    tags = got_rows[:, per_owner : 2 * per_owner, :maxdoc].reshape(devices * per_owner, maxdoc)
    choose = (tags.astype(F32) == indices.astype(F32)[None, :]).astype(BF16)
    return lax.dot_general(
        choose, data, (((0,), (0,)), ((), ())), preferred_element_type=F32
    ).astype(BF16)


def solution(mesh):
    placed = (
        P("dp", "tensor"),
        P("dp", "tensor"),
        P("tensor", None),
        P("tensor", None),
        P("tensor", "dp"),
        P("dp", None),
        P("dp", None),
    )
    return jax.shard_map(
        shards, mesh=mesh, in_specs=placed, out_specs=P("dp", "tensor"), check_vma=False
    )
```

```python
import functools

import jax
import jax.numpy as jnp
from jax import lax
from jax.experimental import pallas as pl
from jax.experimental.pallas import tpu as pltpu
from jax.sharding import PartitionSpec as P


BF16, F32 = jnp.bfloat16, jnp.float32
NT = (((1,), (1,)), ((), ()))
VMEM_LIMIT = 40 << 20


def far(x):
    return pltpu.with_memory_space_constraint(x, pltpu.HBM)


def swap(x, axis, k):
    return lax.ppermute(x, axis, [(i, i ^ k) for i in range(lax.axis_size(axis))])


def project_kernel(per_chunk, ahead, chunk_ref, act_hbm, grad_hbm, wa_hbm, wg_hbm, out_ref, act, grad, wa, wg, sem, wsem):
    blocks, rows = act.shape[0], act.shape[1]

    def copies(i):
        chunk = chunk_ref[i // per_chunk] * per_chunk + i % per_chunk
        at = pl.ds(pl.multiple_of(chunk * rows, rows), rows)
        return (
            pltpu.make_async_copy(grad_hbm.at[at], grad.at[i], sem.at[0, i]),
            pltpu.make_async_copy(act_hbm.at[at], act.at[i], sem.at[1, i]),
        )

    weights = (
        pltpu.make_async_copy(wg_hbm, wg, wsem.at[0]),
        pltpu.make_async_copy(wa_hbm, wa, wsem.at[1]),
    )
    for copy in weights:
        copy.start()
    for i in range(min(ahead, blocks)):
        for copy in copies(i):
            copy.start()
    for copy in weights:
        copy.wait()

    def step(i, carry):
        for copy in copies(i):
            copy.wait()

        @pl.when(i + ahead < blocks)
        def _():
            for copy in copies(i + ahead):
                copy.start()

        left = lax.dot_general(act[i], wa[...], NT, preferred_element_type=F32)
        right = lax.dot_general(grad[i], wg[...], NT, preferred_element_type=F32)
        at = pl.ds(pl.multiple_of(i * rows, rows), rows)
        out_ref[at, :] = jnp.concatenate([left, right], axis=1).astype(out_ref.dtype)
        return carry

    lax.fori_loop(0, blocks, step, 0)


def project(chunks, activations, out_grads, wa, wg, rows, per_chunk, ahead):
    ff, d, k = activations.shape[1], out_grads.shape[1], wa.shape[0]
    count = chunks.shape[0]
    blocks, block = count * per_chunk, rows // per_chunk
    hbm = pl.BlockSpec(memory_space=pl.ANY)
    return pl.pallas_call(
        functools.partial(project_kernel, per_chunk, ahead),
        out_shape=jax.ShapeDtypeStruct((count * rows, 2 * k), BF16),
        in_specs=[pl.BlockSpec(memory_space=pltpu.SMEM)] + [hbm] * 4,
        out_specs=pl.BlockSpec(memory_space=pltpu.VMEM),
        scratch_shapes=[
            pltpu.VMEM((blocks, block, ff), BF16),
            pltpu.VMEM((blocks, block, d), BF16),
            pltpu.VMEM((k, ff), BF16),
            pltpu.VMEM((k, d), BF16),
            pltpu.SemaphoreType.DMA((2, blocks)),
            pltpu.SemaphoreType.DMA((2,)),
        ],
        compiler_params=pltpu.CompilerParams(vmem_limit_bytes=VMEM_LIMIT),
        cost_estimate=pl.CostEstimate(
            flops=2 * count * rows * (ff + d) * k,
            bytes_accessed=2 * count * rows * (ff + d),
            transcendentals=0,
        ),
    )(chunks, far(activations), far(out_grads), far(wa), far(wg))


def score_kernel(n_chunks, group, place_ref, bounds_ref, scale_ref, select_ref, labels_ref, *refs):
    chunks, held = refs[:n_chunks], refs[n_chunks : n_chunks + 2]
    out_ref, left, right, member, sketch, local = refs[n_chunks + 2 :]
    rows, k = chunks[0].shape[0], chunks[0].shape[1] // 2
    docs, nval = bounds_ref.shape[1], local.shape[0]
    for c, ref in enumerate(chunks):
        turned = ref[...].astype(F32).T
        left[:, c * rows : (c + 1) * rows] = turned[:k]
        right[:, c * rows : (c + 1) * rows] = turned[k:].astype(BF16)
        at = place_ref[c] * rows + lax.broadcasted_iota(jnp.int32, (rows, docs), 0)
        inside = (at >= bounds_ref[0:1, :]) & (at < bounds_ref[1:2, :])
        member[c * rows : (c + 1) * rows, :] = inside.astype(F32).astype(BF16)

    def sketch_step(i, carry):
        some = left[pl.ds(pl.multiple_of(i * group, group), group), :].astype(BF16)
        grads = right[...]
        outer = jnp.concatenate([some[j : j + 1, :] * grads for j in range(group)], axis=0)
        summed = jnp.dot(outer, member[...], preferred_element_type=F32)
        at = pl.ds(pl.multiple_of(i * group * k, group * k), group * k)
        sketch[at, :] = (summed * scale_ref[...]).astype(BF16)
        return carry

    lax.fori_loop(0, k // group, sketch_step, 0)
    wide = held[0].shape[1]
    blocks = held[0].shape[0] // nval
    local[...] = jnp.zeros_like(local)
    for half in range(2):

        def local_step(b, carry, half=half):
            start = pl.multiple_of(place_ref[n_chunks + half * blocks + b] * wide, wide)
            local[...] += jnp.dot(
                held[half][pl.ds(pl.multiple_of(b * nval, nval), nval), :],
                sketch[pl.ds(start, wide), :],
                preferred_element_type=F32,
            )
            return carry

        lax.fori_loop(0, blocks, local_step, 0)
    packed = lax.dot_general(
        select_ref[...], local[...].astype(BF16), NT, preferred_element_type=F32
    )
    out_ref[...] = (packed + labels_ref[...]).astype(BF16)


def score(place, bounds, scaling, select, labels, chunks, held, nval):
    tokens = len(chunks) * chunks[0].shape[0]
    k = chunks[0].shape[1] // 2
    docs = bounds.shape[1]
    vmem = pl.BlockSpec(memory_space=pltpu.VMEM)
    return pl.pallas_call(
        functools.partial(score_kernel, len(chunks), 8),
        out_shape=jax.ShapeDtypeStruct((select.shape[0], nval), BF16),
        in_specs=[pl.BlockSpec(memory_space=pltpu.SMEM)] + [vmem] * (4 + len(chunks) + 2),
        out_specs=vmem,
        scratch_shapes=[
            pltpu.VMEM((k, tokens), F32),
            pltpu.VMEM((k, tokens), BF16),
            pltpu.VMEM((tokens, docs), BF16),
            pltpu.VMEM((k * k, docs), BF16),
            pltpu.VMEM((nval, docs), F32),
        ],
        compiler_params=pltpu.CompilerParams(vmem_limit_bytes=16 << 20),
        cost_estimate=pl.CostEstimate(
            flops=2 * k * k * docs * (tokens + nval), bytes_accessed=2 * k * k * nval, transcendentals=0
        ),
        name="score",
    )(place, bounds, scaling, select, labels, *chunks, *held)


def shards(activations, out_grads, proj_in, proj_out, validation, doc_lengths, owner_rows):
    devices, parts = lax.axis_size("dp"), lax.axis_size("tensor")
    me, part = lax.axis_index("dp"), lax.axis_index("tensor")
    tokens, maxdoc = activations.shape[0], doc_lengths.shape[1]
    rows = tokens // parts

    nval = validation.shape[0]
    held, order = validation, [0]
    bits = [1 << i for i in range(devices.bit_length() - 1)]
    for bit in bits[1:]:
        held = jnp.concatenate([held, swap(held, "dp", bit)], axis=0)
        order += [b ^ bit for b in order]
    halves = (held, swap(held, "dp", bits[0]))
    order += [b ^ bits[0] for b in order]

    wa, wg = proj_in.T, proj_out.T
    peers = list(range(parts - 1, 0, -1))
    near = part ^ jnp.array(peers, jnp.int32)
    sent = project(near, activations, out_grads, wa, wg, rows, 1, 2)
    got = [swap(sent[i * rows : (i + 1) * rows], "tensor", peer) for i, peer in enumerate(peers)]
    mine = part + jnp.zeros((1,), jnp.int32)
    mine, _ = lax.optimization_barrier((mine, sent))
    total = project(mine, activations, out_grads, wa, wg, rows, 2, 2).astype(F32)
    for piece in got:
        total = total + piece.astype(F32)
    summed = total.astype(BF16)
    chunks = [summed] + [swap(summed, "tensor", peer) for peer in range(1, parts)]

    lengths, out_rows = doc_lengths[0], owner_rows[0]
    indices = jnp.arange(maxdoc, dtype=jnp.int32)
    starts = jnp.sum(jnp.where(indices[:, None] < indices[None, :], lengths[:, None], 0), axis=0)
    bounds = jnp.stack([starts, starts + lengths])
    scaling = (1.0 / jnp.sqrt(jnp.maximum(lengths, 1).astype(F32)))[None, :]

    per_owner = max(1, maxdoc // devices)
    height = -(-2 * per_owner // 8) * 8
    owners, out_slot = out_rows // maxdoc, out_rows % maxdoc
    earlier = (owners[None, :] == owners[:, None]) & (indices[None, :] < indices[:, None])
    target = owners * height + jnp.sum(earlier.astype(jnp.int32), axis=1)
    at = jnp.arange(devices * height, dtype=jnp.int32)
    select = (target[None, :] == at[:, None]).astype(BF16)
    label = jnp.where(lengths > 0, out_slot, -1)
    labels = jnp.sum(
        jnp.where(target[None, :] + per_owner == at[:, None], label[None, :], 0), axis=1
    )
    labels = jnp.broadcast_to(labels.astype(F32)[:, None], (devices * height, nval))
    place = jnp.concatenate(
        [part ^ jnp.arange(parts, dtype=jnp.int32), me ^ jnp.array(order, jnp.int32)]
    )

    payload = score(place, bounds, scaling, select, labels, chunks, halves, nval)
    got_rows = lax.all_to_all(
        payload.reshape(devices, height, nval), "dp", split_axis=0, concat_axis=0, tiled=True
    )
    data = got_rows[:, :per_owner].reshape(devices * per_owner, nval)
    tags = got_rows[:, per_owner : 2 * per_owner, :maxdoc].reshape(devices * per_owner, maxdoc)
    choose = (tags.astype(F32) == indices.astype(F32)[None, :]).astype(BF16)
    return lax.dot_general(
        choose, data, (((0,), (0,)), ((), ())), preferred_element_type=F32
    ).astype(BF16)


def solution(mesh):
    placed = (
        P("dp", "tensor"),
        P("dp", "tensor"),
        P("tensor", None),
        P("tensor", None),
        P("tensor", "dp"),
        P("dp", None),
        P("dp", None),
    )
    return jax.shard_map(
        shards, mesh=mesh, in_specs=placed, out_specs=P("dp", "tensor"), check_vma=False
    )
```

```python
import functools

import jax
import jax.numpy as jnp
from jax import lax
from jax.experimental import pallas as pl
from jax.experimental.pallas import tpu as pltpu
from jax.sharding import PartitionSpec as P


BF16, F32 = jnp.bfloat16, jnp.float32
NT = (((1,), (1,)), ((), ()))
VMEM_LIMIT = 40 << 20


def far(x):
    return pltpu.with_memory_space_constraint(x, pltpu.HBM)


def swap(x, axis, k):
    return lax.ppermute(x, axis, [(i, i ^ k) for i in range(lax.axis_size(axis))])


def project_kernel(last, per_chunk, ahead, chunk_ref, act_hbm, grad_hbm, wa_hbm, wg_hbm, out_ref, act, grad, wa, wg, sem, wsem):
    blocks, rows = act.shape[0], act.shape[1]

    def copies(i):
        chunk = (chunk_ref[0] ^ (last - i // per_chunk)) * per_chunk + i % per_chunk
        at = pl.ds(pl.multiple_of(chunk * rows, rows), rows)
        return (
            pltpu.make_async_copy(grad_hbm.at[at], grad.at[i], sem.at[0, i]),
            pltpu.make_async_copy(act_hbm.at[at], act.at[i], sem.at[1, i]),
        )

    weights = (
        pltpu.make_async_copy(wg_hbm, wg, wsem.at[0]),
        pltpu.make_async_copy(wa_hbm, wa, wsem.at[1]),
    )
    for copy in weights:
        copy.start()
    for i in range(min(ahead, blocks)):
        for copy in copies(i):
            copy.start()
    for copy in weights:
        copy.wait()

    def step(i, carry):
        for copy in copies(i):
            copy.wait()

        @pl.when(i + ahead < blocks)
        def _():
            for copy in copies(i + ahead):
                copy.start()

        left = lax.dot_general(act[i], wa[...], NT, preferred_element_type=F32)
        right = lax.dot_general(grad[i], wg[...], NT, preferred_element_type=F32)
        at = pl.ds(pl.multiple_of(i % per_chunk * rows, rows), rows)
        out_ref[i // per_chunk, :, at] = jnp.concatenate([left, right], axis=1).T.astype(BF16)
        return carry

    lax.fori_loop(0, blocks, step, 0)


def project(part, last, count, activations, out_grads, wa, wg, rows, per_chunk, ahead):
    ff, d, k = activations.shape[1], out_grads.shape[1], wa.shape[0]
    blocks, block = count * per_chunk, rows // per_chunk
    hbm = pl.BlockSpec(memory_space=pl.ANY)
    return pl.pallas_call(
        functools.partial(project_kernel, last, per_chunk, ahead),
        out_shape=jax.ShapeDtypeStruct((count, 2 * k, rows), BF16),
        in_specs=[pl.BlockSpec(memory_space=pltpu.SMEM)] + [hbm] * 4,
        out_specs=pl.BlockSpec(memory_space=pltpu.VMEM),
        scratch_shapes=[
            pltpu.VMEM((blocks, block, ff), BF16),
            pltpu.VMEM((blocks, block, d), BF16),
            pltpu.VMEM((k, ff), BF16),
            pltpu.VMEM((k, d), BF16),
            pltpu.SemaphoreType.DMA((2, blocks)),
            pltpu.SemaphoreType.DMA((2,)),
        ],
        compiler_params=pltpu.CompilerParams(vmem_limit_bytes=VMEM_LIMIT),
        cost_estimate=pl.CostEstimate(
            flops=2 * count * rows * (ff + d) * k,
            bytes_accessed=2 * count * rows * (ff + d),
            transcendentals=0,
        ),
    )(part, far(activations), far(out_grads), far(wa), far(wg))


def score_kernel(n_chunks, low, place_ref, ends_ref, scale_ref, select_ref, labels_ref, *refs):
    chunks, held = refs[:n_chunks], refs[n_chunks : n_chunks + 2]
    out_ref, left, right, outer, sketch = refs[n_chunks + 2 :]
    k, rows = chunks[0].shape[0] // 2, chunks[0].shape[1]
    high = outer.shape[0] * outer.shape[2] // k
    docs, nval = low * high, out_ref.shape[1]
    for c, ref in enumerate(chunks):
        at = place_ref[c] * rows + lax.broadcasted_iota(jnp.int32, (docs, rows), 1)
        doc = jnp.sum((at >= ends_ref[:, :1]).astype(F32), axis=0, keepdims=True)
        div = jnp.floor(doc * (1.0 / low))
        mod = doc - div * low
        span = slice(c * rows, (c + 1) * rows)
        for m in range(low):
            mask = jnp.broadcast_to((mod == m).astype(F32), (k, rows)).astype(BF16)
            left[m * k : (m + 1) * k, span] = ref[:k, :] * mask
        for m in range(high):
            mask = jnp.broadcast_to((div == m).astype(F32), (k, rows)).astype(BF16)
            right[m * k : (m + 1) * k, span] = ref[k:, :] * mask
    lanes = outer.shape[2]
    sums = lax.dot_general(left[...], right[...], NT, preferred_element_type=F32)
    for m in range(outer.shape[0]):
        outer[m] = sums[:, m * lanes : (m + 1) * lanes]

    first = lax.broadcasted_iota(jnp.int32, (low, lanes), 1) < k
    for m in range(outer.shape[0]):
        scale = scale_ref[:, m * lanes : (m + 1) * lanes]
        for i in range(0, k, 2):
            even = outer[m, pl.ds(i, low, stride=k), :] * scale
            odd = outer[m, pl.ds(i + 1, low, stride=k), :] * scale
            pair = [
                jnp.where(first, even, pltpu.roll(odd, k, 1)),
                jnp.where(first, pltpu.roll(even, k, 1), odd),
            ]
            rows_at = slice(2 * m * low, 2 * (m + 1) * low)
            sketch[rows_at, i * k : i * k + lanes] = jnp.concatenate(pair, axis=0).astype(BF16)

    wide = held[0].shape[1]
    blocks = held[0].shape[0] // nval
    local = jnp.zeros((docs, nval), F32)
    for b in range(2 * blocks):
        start = pl.multiple_of(place_ref[n_chunks + b] * wide, wide)
        at = b % blocks * nval
        local += lax.dot_general(
            sketch[:, pl.ds(start, wide)],
            held[b // blocks][at : at + nval, :],
            NT,
            preferred_element_type=F32,
        )
    packed = jnp.dot(select_ref[...], local.astype(BF16), preferred_element_type=F32)
    out_ref[...] = (packed + labels_ref[...]).astype(BF16)


def score(place, ends, scale, select, labels, chunks, held, nval, low):
    k, rows = chunks[0].shape[0] // 2, chunks[0].shape[1]
    tokens = len(chunks) * rows
    docs = ends.shape[0]
    high = docs // low
    vmem = pl.BlockSpec(memory_space=pltpu.VMEM)
    return pl.pallas_call(
        functools.partial(score_kernel, len(chunks), low),
        out_shape=jax.ShapeDtypeStruct((select.shape[0], nval), BF16),
        in_specs=[pl.BlockSpec(memory_space=pltpu.SMEM)] + [vmem] * (4 + len(chunks) + 2),
        out_specs=vmem,
        scratch_shapes=[
            pltpu.VMEM((low * k, tokens), BF16),
            pltpu.VMEM((high * k, tokens), BF16),
            pltpu.VMEM((high // 2, low * k, 2 * k), F32),
            pltpu.VMEM((docs, k * k), BF16),
        ],
        compiler_params=pltpu.CompilerParams(vmem_limit_bytes=16 << 20),
        cost_estimate=pl.CostEstimate(
            flops=2 * k * k * docs * (tokens + nval), bytes_accessed=2 * k * k * nval, transcendentals=0
        ),
        name="score",
    )(place, ends, scale, select, labels, *chunks, *held)


def shards(activations, out_grads, proj_in, proj_out, validation, doc_lengths, owner_rows):
    devices, parts = lax.axis_size("dp"), lax.axis_size("tensor")
    me, part = lax.axis_index("dp"), lax.axis_index("tensor")
    tokens, maxdoc = activations.shape[0], doc_lengths.shape[1]
    rows = tokens // parts

    nval = validation.shape[0]
    held, order = validation, [0]
    bits = [1 << i for i in range(devices.bit_length() - 1)]
    for bit in bits[1:]:
        held = jnp.concatenate([held, swap(held, "dp", bit)], axis=0)
        order += [b ^ bit for b in order]
    halves = (held, swap(held, "dp", bits[0]))
    order += [b ^ bits[0] for b in order]

    wa, wg = proj_in.T, proj_out.T
    peers = list(range(parts - 1, 0, -1))
    place = part + jnp.zeros((1,), jnp.int32)
    sent = project(place, parts - 1, parts - 1, activations, out_grads, wa, wg, rows, 1, 2)
    got = [swap(sent[i], "tensor", peer) for i, peer in enumerate(peers)]
    place, _ = lax.optimization_barrier((place, sent))
    total = project(place, 0, 1, activations, out_grads, wa, wg, rows, 2, 2)[0].astype(F32)
    for piece in got:
        total = total + piece.astype(F32)
    summed = total.astype(BF16)
    chunks = [summed] + [swap(summed, "tensor", peer) for peer in range(1, parts)]

    lengths, out_rows = doc_lengths[0], owner_rows[0]
    indices = jnp.arange(maxdoc, dtype=jnp.int32)
    starts = jnp.sum(jnp.where(indices[:, None] < indices[None, :], lengths[:, None], 0), axis=0)
    low = maxdoc // 4
    ends = jnp.broadcast_to((starts + lengths)[:, None], (maxdoc, 128))
    scaling = 1.0 / jnp.sqrt(jnp.maximum(lengths, 1).astype(F32))
    scale = jnp.repeat(scaling.reshape(4, low).T, proj_in.shape[1], axis=1)

    per_owner = max(1, maxdoc // devices)
    height = -(-2 * per_owner // 8) * 8
    owners, out_slot = out_rows // maxdoc, out_rows % maxdoc
    earlier = (owners[None, :] == owners[:, None]) & (indices[None, :] < indices[:, None])
    target = owners * height + jnp.sum(earlier.astype(jnp.int32), axis=1)
    at = jnp.arange(devices * height, dtype=jnp.int32)
    select = (target[None, :] == at[:, None]).astype(BF16)
    label = jnp.where(lengths > 0, out_slot, -1)
    labels = jnp.sum(
        jnp.where(target[None, :] + per_owner == at[:, None], label[None, :], 0), axis=1
    )
    labels = jnp.broadcast_to(labels.astype(F32)[:, None], (devices * height, nval))
    place = jnp.concatenate(
        [part ^ jnp.arange(parts, dtype=jnp.int32), me ^ jnp.array(order, jnp.int32)]
    )

    payload = score(place, ends, scale, select, labels, chunks, halves, nval, low)
    got_rows = lax.all_to_all(
        payload.reshape(devices, height, nval), "dp", split_axis=0, concat_axis=0, tiled=True
    )
    data = got_rows[:, :per_owner].reshape(devices * per_owner, nval)
    tags = got_rows[:, per_owner : 2 * per_owner, :maxdoc].reshape(devices * per_owner, maxdoc)
    choose = (tags.astype(F32) == indices.astype(F32)[None, :]).astype(BF16)
    return lax.dot_general(
        choose, data, (((0,), (0,)), ((), ())), preferred_element_type=F32
    ).astype(BF16)


def solution(mesh):
    placed = (
        P("dp", "tensor"),
        P("dp", "tensor"),
        P("tensor", None),
        P("tensor", None),
        P("tensor", "dp"),
        P("dp", None),
        P("dp", None),
    )
    return jax.shard_map(
        shards, mesh=mesh, in_specs=placed, out_specs=P("dp", "tensor"), check_vma=False
    )
```

```python
import functools

import jax
import jax.numpy as jnp
from jax import lax
from jax.experimental import pallas as pl
from jax.experimental.pallas import tpu as pltpu
from jax.sharding import PartitionSpec as P


BF16, F32 = jnp.bfloat16, jnp.float32
NT = (((1,), (1,)), ((), ()))
VMEM_LIMIT = 24 << 20


def far(x):
    return pltpu.with_memory_space_constraint(x, pltpu.HBM)


def swap(x, axis, k):
    return lax.ppermute(x, axis, [(i, i ^ k) for i in range(lax.axis_size(axis))])


def both_projections(act, grad, wa, wg):
    left = lax.dot_general(act, wa, NT, preferred_element_type=F32)
    right = lax.dot_general(grad, wg, NT, preferred_element_type=F32)
    return jnp.concatenate([left, right], axis=1).T.astype(BF16)


def peers_kernel(
    ahead, act_hbm, grad_hbm, wa_hbm, wg_hbm, out_ref, grad_own, wa, wg, act, grad, sem, wsem
):
    count, rows = act.shape[0], act.shape[1]
    part = lax.axis_index("tensor")

    def rows_of(chunk):
        return pl.ds(pl.multiple_of(chunk * rows, rows), rows)

    def copies(i):
        at = rows_of(part ^ (count - i))
        return (
            pltpu.make_async_copy(grad_hbm.at[at], grad.at[i], sem.at[0, i]),
            pltpu.make_async_copy(act_hbm.at[at], act.at[i], sem.at[1, i]),
        )

    weights = (
        pltpu.make_async_copy(wg_hbm, wg, wsem.at[0]),
        pltpu.make_async_copy(wa_hbm, wa, wsem.at[1]),
    )
    own = pltpu.make_async_copy(grad_hbm.at[rows_of(part)], grad_own, wsem.at[2])
    for copy in weights:
        copy.start()
    for i in range(min(ahead, count)):
        for copy in copies(i):
            copy.start()
    for copy in weights:
        copy.wait()

    def step(i, carry):
        for copy in copies(i):
            copy.wait()

        @pl.when(i + ahead < count)
        def _():
            for copy in copies(i + ahead):
                copy.start()

        @pl.when(i + ahead == count)
        def _():
            own.start()

        out_ref[i] = both_projections(act[i], grad[i], wa[...], wg[...])
        return carry

    lax.fori_loop(0, count, step, 0)
    own.wait()


def project_peers(parts, activations, out_grads, wa, wg):
    (tokens, ff), d, k = activations.shape, out_grads.shape[1], wa.shape[0]
    rows, count = tokens // parts, parts - 1
    hbm, vmem = pl.BlockSpec(memory_space=pl.ANY), pl.BlockSpec(memory_space=pltpu.VMEM)
    return pl.pallas_call(
        functools.partial(peers_kernel, min(2, count)),
        out_shape=[
            jax.ShapeDtypeStruct(shape, BF16)
            for shape in ((count, 2 * k, rows), (rows, d), (k, ff), (k, d))
        ],
        in_specs=[hbm] * 4,
        out_specs=[vmem] * 4,
        scratch_shapes=[
            pltpu.VMEM((count, rows, ff), BF16),
            pltpu.VMEM((count, rows, d), BF16),
            pltpu.SemaphoreType.DMA((2, count)),
            pltpu.SemaphoreType.DMA((3,)),
        ],
        compiler_params=pltpu.CompilerParams(vmem_limit_bytes=VMEM_LIMIT),
        cost_estimate=pl.CostEstimate(
            flops=2 * tokens * (ff + d) * k, bytes_accessed=2 * tokens * (ff + d), transcendentals=0
        ),
        name="project_peers",
    )(far(activations), far(out_grads), far(wa), far(wg))


def own_kernel(act_hbm, grad_ref, wa_ref, wg_ref, out_ref, act, sem):
    blocks, rows = act.shape[0], act.shape[1]
    part = lax.axis_index("tensor")

    def copy(i):
        start = pl.multiple_of((part * blocks + i) * rows, rows)
        return pltpu.make_async_copy(act_hbm.at[pl.ds(start, rows)], act.at[i], sem.at[i])

    for i in range(blocks):
        copy(i).start()

    def step(i, carry):
        copy(i).wait()
        at = pl.ds(pl.multiple_of(i * rows, rows), rows)
        out_ref[:, at] = both_projections(act[i], grad_ref[at, :], wa_ref[...], wg_ref[...])
        return carry

    lax.fori_loop(0, blocks, step, 0)


def project_own(activations, grad, wa, wg, blocks):
    hbm, vmem = pl.BlockSpec(memory_space=pl.ANY), pl.BlockSpec(memory_space=pltpu.VMEM)
    ff, (rows, d), k = activations.shape[1], grad.shape, wa.shape[0]
    return pl.pallas_call(
        own_kernel,
        out_shape=jax.ShapeDtypeStruct((2 * k, rows), BF16),
        in_specs=[hbm] + [vmem] * 3,
        out_specs=vmem,
        scratch_shapes=[
            pltpu.VMEM((blocks, rows // blocks, ff), BF16),
            pltpu.SemaphoreType.DMA((blocks,)),
        ],
        compiler_params=pltpu.CompilerParams(vmem_limit_bytes=VMEM_LIMIT),
        cost_estimate=pl.CostEstimate(
            flops=2 * rows * (ff + d) * k, bytes_accessed=2 * rows * (ff + d), transcendentals=0
        ),
        name="project_own",
    )(far(activations), grad, wa, wg)


def score_kernel(n_chunks, low, n_blocks, ends_ref, scale_ref, select_ref, labels_ref, *refs):
    chunks, held = refs[:n_chunks], refs[n_chunks : n_chunks + 2]
    out_ref, acts, left, right, outer, sketch = refs[n_chunks + 2 :]
    k, rows = chunks[0].shape[0] // 2, chunks[0].shape[1]
    high = outer.shape[0] * outer.shape[2] // k
    docs = low * high
    part, me = lax.axis_index("tensor"), lax.axis_index("dp")
    for c, ref in enumerate(chunks):
        at = (part ^ c) * rows + lax.broadcasted_iota(jnp.int32, (docs, rows), 1)
        doc = jnp.sum((at >= ends_ref[:, :1]).astype(F32), axis=0, keepdims=True)
        div = jnp.floor(doc * (1.0 / low))
        of_mod = lax.broadcasted_iota(jnp.int32, (low, rows), 0).astype(F32)
        mod = (jnp.broadcast_to(doc - div * low, (low, rows)) == of_mod).astype(F32)
        span = slice(c * rows, (c + 1) * rows)
        acts[...] = ref[:k, :].astype(F32)
        for i in range(0, k, 2):
            pair = [jnp.broadcast_to(acts[j : j + 1, :], (low, rows)) * mod for j in (i, i + 1)]
            left[i * low : (i + 2) * low, span] = jnp.concatenate(pair, axis=0).astype(BF16)
        for m in range(high):
            mask = jnp.broadcast_to((div == m).astype(F32), (k, rows)).astype(BF16)
            right[m * k : (m + 1) * k, span] = ref[k:, :] * mask
    lanes = outer.shape[2]
    sums = lax.dot_general(left[...], right[...], NT, preferred_element_type=F32)
    for m in range(outer.shape[0]):
        outer[m] = sums[:, m * lanes : (m + 1) * lanes]

    first = lax.broadcasted_iota(jnp.int32, (low, lanes), 1) < k
    per_block = k // n_blocks
    for m in range(outer.shape[0]):
        scale = scale_ref[:, m * lanes : (m + 1) * lanes]
        for i in range(0, k, 2):
            even = outer[m, i * low : (i + 1) * low, :] * scale
            odd = outer[m, (i + 1) * low : (i + 2) * low, :] * scale
            pair = [
                jnp.where(first, even, pltpu.roll(odd, k, 1)),
                jnp.where(first, pltpu.roll(even, k, 1), odd),
            ]
            apart = me ^ (i // per_block)
            at = (apart // 2 + apart % 2 * (n_blocks // 2)) * (per_block * k) + i % per_block * k
            rows_at = slice(2 * m * low, 2 * (m + 1) * low)
            sketch[rows_at, pl.ds(pl.multiple_of(at, lanes), lanes)] = jnp.concatenate(pair, axis=0).astype(BF16)

    half = held[0].shape[1]
    local = sum(
        lax.dot_general(
            ref[...], sketch[:, h * half : (h + 1) * half], NT, preferred_element_type=F32
        )
        for h, ref in enumerate(held)
    )
    packed = lax.dot_general(
        select_ref[...], local.astype(BF16), NT, preferred_element_type=F32
    )
    out_ref[...] = (packed + labels_ref[...]).astype(BF16)


def score(ends, scale, select, labels, chunks, held, nval, low, n_blocks):
    k, rows = chunks[0].shape[0] // 2, chunks[0].shape[1]
    tokens = len(chunks) * rows
    docs = ends.shape[0]
    high = docs // low
    vmem = pl.BlockSpec(memory_space=pltpu.VMEM)
    return pl.pallas_call(
        functools.partial(score_kernel, len(chunks), low, n_blocks),
        out_shape=jax.ShapeDtypeStruct((select.shape[0], nval), BF16),
        in_specs=[vmem] * (4 + len(chunks) + 2),
        out_specs=vmem,
        scratch_shapes=[
            pltpu.VMEM((k, rows), F32),
            pltpu.VMEM((low * k, tokens), BF16),
            pltpu.VMEM((high * k, tokens), BF16),
            pltpu.VMEM((high // 2, low * k, 2 * k), F32),
            pltpu.VMEM((docs, k * k), BF16),
        ],
        compiler_params=pltpu.CompilerParams(vmem_limit_bytes=16 << 20),
        cost_estimate=pl.CostEstimate(
            flops=2 * k * k * docs * (tokens + nval), bytes_accessed=2 * k * k * nval, transcendentals=0
        ),
        name="score",
    )(ends, scale, select, labels, *chunks, *held)


def shards(activations, out_grads, proj_in, proj_out, validation, doc_lengths, owner_rows):
    devices, parts = lax.axis_size("dp"), lax.axis_size("tensor")
    maxdoc = doc_lengths.shape[1]

    nval = validation.shape[0]
    held = validation
    bits = [1 << i for i in range(devices.bit_length() - 1)]
    for bit in bits[1:]:
        held = jnp.concatenate([held, swap(held, "dp", bit)], axis=1)
    halves = (held, swap(held, "dp", bits[0]))

    wa, wg = proj_in.T, proj_out.T
    peers = list(range(parts - 1, 0, -1))
    sent, *kept = project_peers(parts, activations, out_grads, wa, wg)
    got = [swap(sent[i], "tensor", peer) for i, peer in enumerate(peers)]
    total = project_own(activations, *kept, 2).astype(F32)
    for piece in got:
        total = total + piece.astype(F32)
    summed = total.astype(BF16)
    summed, lengths, out_rows = lax.optimization_barrier((summed, doc_lengths[0], owner_rows[0]))
    chunks = [summed] + [swap(summed, "tensor", peer) for peer in range(1, parts)]

    indices = jnp.arange(maxdoc, dtype=jnp.int32)
    starts = jnp.sum(jnp.where(indices[:, None] < indices[None, :], lengths[:, None], 0), axis=0)
    low = maxdoc // 4
    ends = jnp.broadcast_to((starts + lengths)[:, None], (maxdoc, 128))
    scaling = 1.0 / jnp.sqrt(jnp.maximum(lengths, 1).astype(F32))
    scale = jnp.repeat(scaling.reshape(4, low).T, proj_in.shape[1], axis=1)

    per_owner = max(1, maxdoc // devices)
    height = -(-2 * per_owner // 8) * 8
    owners, out_slot = out_rows // maxdoc, out_rows % maxdoc
    earlier = (owners[None, :] == owners[:, None]) & (indices[None, :] < indices[:, None])
    target = owners * height + jnp.sum(earlier.astype(jnp.int32), axis=1)
    at = jnp.arange(devices * height, dtype=jnp.int32)
    select = (target[None, :] == at[:, None]).astype(BF16)
    label = jnp.where(lengths > 0, out_slot, -1)
    labels = jnp.sum(
        jnp.where(target[None, :] + per_owner == at[:, None], label[None, :], 0), axis=1
    )
    labels = jnp.broadcast_to(labels.astype(F32)[:, None], (devices * height, nval))

    payload = score(ends, scale, select, labels, chunks, halves, nval, low, devices)
    got_rows = lax.all_to_all(
        payload.reshape(devices, height, nval), "dp", split_axis=0, concat_axis=0, tiled=True
    )
    data = got_rows[:, :per_owner].reshape(devices * per_owner, nval)
    tags = got_rows[:, per_owner : 2 * per_owner, :maxdoc].reshape(devices * per_owner, maxdoc)
    choose = (tags.astype(F32) == indices.astype(F32)[None, :]).astype(BF16)
    return lax.dot_general(
        choose, data, (((0,), (0,)), ((), ())), preferred_element_type=F32
    ).astype(BF16)


def solution(mesh):
    placed = (
        P("dp", "tensor"),
        P("dp", "tensor"),
        P("tensor", None),
        P("tensor", None),
        P("tensor", "dp"),
        P("dp", None),
        P("dp", None),
    )
    return jax.shard_map(
        shards, mesh=mesh, in_specs=placed, out_specs=P("dp", "tensor"), check_vma=False
    )
```

```python
import functools

import jax
import jax.numpy as jnp
from jax import lax
from jax.experimental import pallas as pl
from jax.experimental.pallas import tpu as pltpu
from jax.sharding import PartitionSpec as P


BF16, F32 = jnp.bfloat16, jnp.float32
NT = (((1,), (1,)), ((), ()))
VMEM_LIMIT = 24 << 20


def far(x):
    return pltpu.with_memory_space_constraint(x, pltpu.HBM)


def swap(x, axis, k):
    return lax.ppermute(x, axis, [(i, i ^ k) for i in range(lax.axis_size(axis))])


def both_projections(act, grad, wa, wg):
    left = lax.dot_general(act, wa, NT, preferred_element_type=F32)
    right = lax.dot_general(grad, wg, NT, preferred_element_type=F32)
    return jnp.concatenate([left, right], axis=1).T.astype(BF16)


def peers_kernel(
    ahead, act_hbm, grad_hbm, wa_hbm, wg_hbm, out_ref, grad_own, wa, wg, act, grad, sem, wsem
):
    count, rows = act.shape[0], act.shape[1]
    part = lax.axis_index("tensor")

    def rows_of(chunk):
        return pl.ds(pl.multiple_of(chunk * rows, rows), rows)

    def act_copies(at, i):
        wide = act.shape[2] // 2
        return [
            pltpu.make_async_copy(
                act_hbm.at[at, pl.ds(j * wide, wide)], act.at[i, :, pl.ds(j * wide, wide)], sem.at[1 + j, i]
            )
            for j in range(2)
        ]

    def copies(i):
        at = rows_of(part ^ (count - i))
        return (
            pltpu.make_async_copy(grad_hbm.at[at], grad.at[i], sem.at[0, i]),
            *act_copies(at, i),
        )

    weights = (
        pltpu.make_async_copy(wg_hbm, wg, wsem.at[0]),
        pltpu.make_async_copy(wa_hbm, wa, wsem.at[1]),
    )
    own = pltpu.make_async_copy(grad_hbm.at[rows_of(part)], grad_own, wsem.at[2])
    for copy in weights:
        copy.start()
    for copy in copies(0):
        copy.start()
    for copy in weights:
        copy.wait()
    for i in range(1, min(ahead, count)):
        for copy in copies(i):
            copy.start()

    def step(i, carry):
        for copy in copies(i):
            copy.wait()

        @pl.when(i + ahead < count)
        def _():
            for copy in copies(i + ahead):
                copy.start()

        @pl.when(i + ahead == count)
        def _():
            own.start()

        out_ref[i] = both_projections(act[i], grad[i], wa[...], wg[...])
        return carry

    lax.fori_loop(0, count, step, 0)
    own.wait()


def project_peers(parts, activations, out_grads, wa, wg):
    (tokens, ff), d, k = activations.shape, out_grads.shape[1], wa.shape[0]
    rows, count = tokens // parts, parts - 1
    hbm, vmem = pl.BlockSpec(memory_space=pl.ANY), pl.BlockSpec(memory_space=pltpu.VMEM)
    return pl.pallas_call(
        functools.partial(peers_kernel, min(2, count)),
        out_shape=[
            jax.ShapeDtypeStruct(shape, BF16)
            for shape in ((count, 2 * k, rows), (rows, d), (k, ff), (k, d))
        ],
        in_specs=[hbm] * 4,
        out_specs=[vmem] * 4,
        scratch_shapes=[
            pltpu.VMEM((count, rows, ff), BF16),
            pltpu.VMEM((count, rows, d), BF16),
            pltpu.SemaphoreType.DMA((3, count)),
            pltpu.SemaphoreType.DMA((3,)),
        ],
        compiler_params=pltpu.CompilerParams(vmem_limit_bytes=VMEM_LIMIT),
        cost_estimate=pl.CostEstimate(
            flops=2 * tokens * (ff + d) * k, bytes_accessed=2 * tokens * (ff + d), transcendentals=0
        ),
        name="project_peers",
    )(far(activations), far(out_grads), far(wa), far(wg))


def own_kernel(act_hbm, grad_ref, wa_ref, wg_ref, out_ref, act, sem):
    blocks, rows = act.shape[0], act.shape[1]
    part = lax.axis_index("tensor")

    def copy(i):
        start = pl.multiple_of((part * blocks + i) * rows, rows)
        return pltpu.make_async_copy(act_hbm.at[pl.ds(start, rows)], act.at[i], sem.at[i])

    for i in range(blocks):
        copy(i).start()

    def step(i, carry):
        copy(i).wait()
        at = pl.ds(pl.multiple_of(i * rows, rows), rows)
        out_ref[:, at] = both_projections(act[i], grad_ref[at, :], wa_ref[...], wg_ref[...])
        return carry

    lax.fori_loop(0, blocks, step, 0)


def project_own(activations, grad, wa, wg, blocks):
    hbm, vmem = pl.BlockSpec(memory_space=pl.ANY), pl.BlockSpec(memory_space=pltpu.VMEM)
    ff, (rows, d), k = activations.shape[1], grad.shape, wa.shape[0]
    return pl.pallas_call(
        own_kernel,
        out_shape=jax.ShapeDtypeStruct((2 * k, rows), BF16),
        in_specs=[hbm] + [vmem] * 3,
        out_specs=vmem,
        scratch_shapes=[
            pltpu.VMEM((blocks, rows // blocks, ff), BF16),
            pltpu.SemaphoreType.DMA((blocks,)),
        ],
        compiler_params=pltpu.CompilerParams(vmem_limit_bytes=VMEM_LIMIT),
        cost_estimate=pl.CostEstimate(
            flops=2 * rows * (ff + d) * k, bytes_accessed=2 * rows * (ff + d), transcendentals=0
        ),
        name="project_own",
    )(far(activations), grad, wa, wg)


def score_kernel(n_chunks, low, n_blocks, ends_ref, scale_ref, select_ref, labels_ref, *refs):
    chunks, held = refs[:n_chunks], refs[n_chunks : n_chunks + 2]
    near_ref, far_ref, acts, left, right, outer, sketch = refs[n_chunks + 2 :]
    k, rows = chunks[0].shape[0] // 2, chunks[0].shape[1]
    high = outer.shape[0] * outer.shape[2] // k
    docs = low * high
    part, me = lax.axis_index("tensor"), lax.axis_index("dp")
    for c, ref in enumerate(chunks):
        at = (part ^ c) * rows + lax.broadcasted_iota(jnp.int32, (docs, rows), 1)
        doc = jnp.sum((at >= ends_ref[:, :1]).astype(F32), axis=0, keepdims=True)
        div = jnp.floor(doc * (1.0 / low))
        of_mod = lax.broadcasted_iota(jnp.int32, (low, rows), 0).astype(F32)
        mod = (jnp.broadcast_to(doc - div * low, (low, rows)) == of_mod).astype(F32)
        span = slice(c * rows, (c + 1) * rows)
        acts[...] = ref[:k, :].astype(F32)
        for i in range(0, k, 2):
            pair = [jnp.broadcast_to(acts[j : j + 1, :], (low, rows)) * mod for j in (i, i + 1)]
            left[i * low : (i + 2) * low, span] = jnp.concatenate(pair, axis=0).astype(BF16)
        for m in range(high):
            mask = jnp.broadcast_to((div == m).astype(F32), (k, rows)).astype(BF16)
            right[m * k : (m + 1) * k, span] = ref[k:, :] * mask
    lanes = outer.shape[2]
    sums = lax.dot_general(left[...], right[...], NT, preferred_element_type=F32)
    for m in range(outer.shape[0]):
        outer[m] = sums[:, m * lanes : (m + 1) * lanes]

    first = lax.broadcasted_iota(jnp.int32, (low, lanes), 1) < k
    per_block = k // n_blocks
    for m in range(outer.shape[0]):
        scale = scale_ref[:, m * lanes : (m + 1) * lanes]
        for i in range(0, k, 2):
            even = outer[m, i * low : (i + 1) * low, :] * scale
            odd = outer[m, (i + 1) * low : (i + 2) * low, :] * scale
            pair = [
                jnp.where(first, even, pltpu.roll(odd, k, 1)),
                jnp.where(first, pltpu.roll(even, k, 1), odd),
            ]
            apart = me ^ (i // per_block)
            at = (apart // 2 + apart % 2 * (n_blocks // 2)) * (per_block * k) + i % per_block * k
            rows_at = slice(2 * m * low, 2 * (m + 1) * low)
            sketch[rows_at, pl.ds(pl.multiple_of(at, lanes), lanes)] = jnp.concatenate(pair, axis=0).astype(BF16)

    half = held[0].shape[1]
    local = sum(
        lax.dot_general(
            ref[...], sketch[:, h * half : (h + 1) * half], NT, preferred_element_type=F32
        )
        for h, ref in enumerate(held)
    )
    packed = lax.dot_general(
        select_ref[...], local.astype(BF16), NT, preferred_element_type=F32
    )
    packed = (packed + labels_ref[...]).astype(BF16)
    near_ref[...], far_ref[...] = packed[: near_ref.shape[0]], packed[near_ref.shape[0] :]


def score(ends, scale, select, labels, chunks, held, nval, low, n_blocks):
    k, rows = chunks[0].shape[0] // 2, chunks[0].shape[1]
    tokens = len(chunks) * rows
    docs = ends.shape[0]
    high = docs // low
    vmem = pl.BlockSpec(memory_space=pltpu.VMEM)
    return pl.pallas_call(
        functools.partial(score_kernel, len(chunks), low, n_blocks),
        out_shape=[jax.ShapeDtypeStruct((select.shape[0] // 2, nval), BF16)] * 2,
        in_specs=[vmem] * (4 + len(chunks) + 2),
        out_specs=[vmem] * 2,
        scratch_shapes=[
            pltpu.VMEM((k, rows), F32),
            pltpu.VMEM((low * k, tokens), BF16),
            pltpu.VMEM((high * k, tokens), BF16),
            pltpu.VMEM((high // 2, low * k, 2 * k), F32),
            pltpu.VMEM((docs, k * k), BF16),
        ],
        compiler_params=pltpu.CompilerParams(vmem_limit_bytes=16 << 20),
        cost_estimate=pl.CostEstimate(
            flops=2 * k * k * docs * (tokens + nval), bytes_accessed=2 * k * k * nval, transcendentals=0
        ),
        name="score",
    )(ends, scale, select, labels, *chunks, *held)


def shards(activations, out_grads, proj_in, proj_out, validation, doc_lengths, owner_rows):
    devices, parts = lax.axis_size("dp"), lax.axis_size("tensor")
    maxdoc = doc_lengths.shape[1]

    nval = validation.shape[0]
    held = validation
    bits = [1 << i for i in range(devices.bit_length() - 1)]
    for bit in bits[1:]:
        held = jnp.concatenate([held, swap(held, "dp", bit)], axis=1)
    halves = (held, swap(held, "dp", bits[0]))

    wa, wg = proj_in.T, proj_out.T
    peers = list(range(parts - 1, 0, -1))
    sent, *kept = project_peers(parts, activations, out_grads, wa, wg)
    got = [swap(sent[i], "tensor", peer) for i, peer in enumerate(peers)]
    total = project_own(activations, *kept, 2).astype(F32)
    for piece in got:
        total = total + piece.astype(F32)
    summed = total.astype(BF16)
    summed, lengths, out_rows = lax.optimization_barrier((summed, doc_lengths[0], owner_rows[0]))
    chunks = [summed] + [swap(summed, "tensor", peer) for peer in range(1, parts)]

    indices = jnp.arange(maxdoc, dtype=jnp.int32)
    starts = jnp.sum(jnp.where(indices[:, None] < indices[None, :], lengths[:, None], 0), axis=0)
    low = maxdoc // 4
    ends = jnp.broadcast_to((starts + lengths)[:, None], (maxdoc, 128))
    scaling = 1.0 / jnp.sqrt(jnp.maximum(lengths, 1).astype(F32))
    scale = jnp.repeat(scaling.reshape(4, low).T, proj_in.shape[1], axis=1)

    per_owner = max(1, maxdoc // devices)
    height = -(-2 * per_owner // 8) * 8
    owners, out_slot = out_rows // maxdoc, out_rows % maxdoc
    earlier = (owners[None, :] == owners[:, None]) & (indices[None, :] < indices[:, None])
    within = jnp.sum(earlier.astype(jnp.int32), axis=1)
    apart = owners ^ lax.axis_index("dp")
    target = (apart // 2 + apart % 2 * (devices // 2)) * height + within
    at = jnp.arange(devices * height, dtype=jnp.int32)
    select = (target[None, :] == at[:, None]).astype(BF16)
    label = jnp.where(lengths > 0, out_slot, -1)
    labels = jnp.sum(
        jnp.where(target[None, :] + per_owner == at[:, None], label[None, :], 0), axis=1
    )
    labels = jnp.broadcast_to(labels.astype(F32)[:, None], (devices * height, nval))

    near, away = score(ends, scale, select, labels, chunks, halves, nval, low, devices)
    crossed = swap(away, "dp", 1)
    blocks = [slice(i * height, (i + 1) * height) for i in range(devices // 2)]
    rows = [jnp.concatenate([near[at], crossed[at]], axis=0) for at in blocks]
    rows = rows[:1] + [swap(rows[i], "dp", 2 * i) for i in range(1, devices // 2)]
    got_rows = jnp.concatenate(rows, axis=0).reshape(devices, height, nval)
    data = got_rows[:, :per_owner].reshape(devices * per_owner, nval)
    tags = got_rows[:, per_owner : 2 * per_owner, :maxdoc].reshape(devices * per_owner, maxdoc)
    choose = (tags.astype(F32) == indices.astype(F32)[None, :]).astype(BF16)
    return lax.dot_general(
        choose, data, (((0,), (0,)), ((), ())), preferred_element_type=F32
    ).astype(BF16)


def solution(mesh):
    placed = (
        P("dp", "tensor"),
        P("dp", "tensor"),
        P("tensor", None),
        P("tensor", None),
        P("tensor", "dp"),
        P("dp", None),
        P("dp", None),
    )
    return jax.shard_map(
        shards, mesh=mesh, in_specs=placed, out_specs=P("dp", "tensor"), check_vma=False
    )
```

```python
import functools

import jax
import jax.numpy as jnp
from jax import lax
from jax.experimental import pallas as pl
from jax.experimental.pallas import tpu as pltpu
from jax.sharding import PartitionSpec as P


BF16, F32 = jnp.bfloat16, jnp.float32
NT = (((1,), (1,)), ((), ()))
VMEM_LIMIT = 24 << 20


def far(x):
    return pltpu.with_memory_space_constraint(x, pltpu.HBM)


def swap(x, axis, k):
    return lax.ppermute(x, axis, [(i, i ^ k) for i in range(lax.axis_size(axis))])


def both_projections(act, grad, wa, wg):
    left = lax.dot_general(act, wa, NT, preferred_element_type=F32)
    right = lax.dot_general(grad, wg, NT, preferred_element_type=F32)
    return jnp.concatenate([left, right], axis=1).T.astype(BF16)


def peers_kernel(
    ahead, act_hbm, grad_hbm, wa_hbm, wg_hbm, out_ref, grad_own, wa, wg, act, grad, sem, wsem
):
    count, rows = act.shape[0], act.shape[1]
    part = lax.axis_index("tensor")

    def rows_of(chunk):
        return pl.ds(pl.multiple_of(chunk * rows, rows), rows)

    def act_copies(at, i):
        wide = act.shape[2] // 2
        return [
            pltpu.make_async_copy(
                act_hbm.at[at, pl.ds(j * wide, wide)], act.at[i, :, pl.ds(j * wide, wide)], sem.at[1 + j, i]
            )
            for j in range(2)
        ]

    def copies(i):
        at = rows_of(part ^ (count - i))
        return (
            pltpu.make_async_copy(grad_hbm.at[at], grad.at[i], sem.at[0, i]),
            *act_copies(at, i),
        )

    weights = (
        pltpu.make_async_copy(wg_hbm, wg, wsem.at[0]),
        pltpu.make_async_copy(wa_hbm, wa, wsem.at[1]),
    )
    own = pltpu.make_async_copy(grad_hbm.at[rows_of(part)], grad_own, wsem.at[2])
    for copy in weights:
        copy.start()
    for copy in copies(0):
        copy.start()
    for copy in weights:
        copy.wait()
    for i in range(1, min(ahead, count)):
        for copy in copies(i):
            copy.start()

    def step(i, carry):
        for copy in copies(i):
            copy.wait()

        @pl.when(i + ahead < count)
        def _():
            for copy in copies(i + ahead):
                copy.start()

        @pl.when(i + ahead == count)
        def _():
            own.start()

        out_ref[i] = both_projections(act[i], grad[i], wa[...], wg[...])
        return carry

    lax.fori_loop(0, count, step, 0)
    own.wait()


def project_peers(parts, activations, out_grads, wa, wg):
    (tokens, ff), d, k = activations.shape, out_grads.shape[1], wa.shape[0]
    rows, count = tokens // parts, parts - 1
    hbm, vmem = pl.BlockSpec(memory_space=pl.ANY), pl.BlockSpec(memory_space=pltpu.VMEM)
    return pl.pallas_call(
        functools.partial(peers_kernel, min(2, count)),
        out_shape=[
            jax.ShapeDtypeStruct(shape, BF16)
            for shape in ((count, 2 * k, rows), (rows, d), (k, ff), (k, d))
        ],
        in_specs=[hbm] * 4,
        out_specs=[vmem] * 4,
        scratch_shapes=[
            pltpu.VMEM((count, rows, ff), BF16),
            pltpu.VMEM((count, rows, d), BF16),
            pltpu.SemaphoreType.DMA((3, count)),
            pltpu.SemaphoreType.DMA((3,)),
        ],
        compiler_params=pltpu.CompilerParams(vmem_limit_bytes=VMEM_LIMIT),
        cost_estimate=pl.CostEstimate(
            flops=2 * tokens * (ff + d) * k, bytes_accessed=2 * tokens * (ff + d), transcendentals=0
        ),
        name="project_peers",
    )(far(activations), far(out_grads), far(wa), far(wg))


def own_kernel(act_hbm, grad_ref, wa_ref, wg_ref, out_ref, act, sem):
    blocks, rows = act.shape[0], act.shape[1]
    part = lax.axis_index("tensor")

    def copy(i):
        start = pl.multiple_of((part * blocks + i) * rows, rows)
        return pltpu.make_async_copy(act_hbm.at[pl.ds(start, rows)], act.at[i], sem.at[i])

    for i in range(blocks):
        copy(i).start()

    def step(i, carry):
        copy(i).wait()
        at = pl.ds(pl.multiple_of(i * rows, rows), rows)
        out_ref[:, at] = both_projections(act[i], grad_ref[at, :], wa_ref[...], wg_ref[...])
        return carry

    lax.fori_loop(0, blocks, step, 0)


def project_own(activations, grad, wa, wg, blocks):
    hbm, vmem = pl.BlockSpec(memory_space=pl.ANY), pl.BlockSpec(memory_space=pltpu.VMEM)
    ff, (rows, d), k = activations.shape[1], grad.shape, wa.shape[0]
    return pl.pallas_call(
        own_kernel,
        out_shape=jax.ShapeDtypeStruct((2 * k, rows), BF16),
        in_specs=[hbm] + [vmem] * 3,
        out_specs=vmem,
        scratch_shapes=[
            pltpu.VMEM((blocks, rows // blocks, ff), BF16),
            pltpu.SemaphoreType.DMA((blocks,)),
        ],
        compiler_params=pltpu.CompilerParams(vmem_limit_bytes=VMEM_LIMIT),
        cost_estimate=pl.CostEstimate(
            flops=2 * rows * (ff + d) * k, bytes_accessed=2 * rows * (ff + d), transcendentals=0
        ),
        name="project_own",
    )(far(activations), grad, wa, wg)


def outer_sums(offsets, low, ends_ref, chunks, acts, left, right):
    k, rows = chunks[0].shape[0] // 2, chunks[0].shape[1]
    docs, high = ends_ref.shape[0], right.shape[0] // k
    part = lax.axis_index("tensor")
    for c, ref in enumerate(chunks):
        at = (part ^ offsets[c]) * rows + lax.broadcasted_iota(jnp.int32, (docs, rows), 1)
        doc = jnp.sum((at >= ends_ref[:, :1]).astype(F32), axis=0, keepdims=True)
        div = jnp.floor(doc * (1.0 / low))
        of_mod = lax.broadcasted_iota(jnp.int32, (low, rows), 0).astype(F32)
        mod = (jnp.broadcast_to(doc - div * low, (low, rows)) == of_mod).astype(F32)
        span = slice(c * rows, (c + 1) * rows)
        acts[...] = ref[:k, :].astype(F32)
        for i in range(0, k, 2):
            pair = [jnp.broadcast_to(acts[j : j + 1, :], (low, rows)) * mod for j in (i, i + 1)]
            left[i * low : (i + 2) * low, span] = jnp.concatenate(pair, axis=0).astype(BF16)
        for m in range(high):
            mask = jnp.broadcast_to((div == m).astype(F32), (k, rows)).astype(BF16)
            right[m * k : (m + 1) * k, span] = ref[k:, :] * mask
    return lax.dot_general(left[...], right[...], NT, preferred_element_type=F32)


def sums_scratch(count, k, rows, low, high):
    return [
        pltpu.VMEM((k, rows), F32),
        pltpu.VMEM((low * k, count * rows), BF16),
        pltpu.VMEM((high * k, count * rows), BF16),
    ]


def early_kernel(offsets, low, ends_ref, *refs):
    *chunks, out_ref, acts, left, right = refs
    out_ref[...] = outer_sums(offsets, low, ends_ref, chunks, acts, left, right)


def early_sums(offsets, ends, chunks, low):
    vmem = pl.BlockSpec(memory_space=pltpu.VMEM)
    k, rows = chunks[0].shape[0] // 2, chunks[0].shape[1]
    high = ends.shape[0] // low
    return pl.pallas_call(
        functools.partial(early_kernel, offsets, low),
        out_shape=jax.ShapeDtypeStruct((low * k, high * k), F32),
        in_specs=[vmem] * (1 + len(chunks)),
        out_specs=vmem,
        scratch_shapes=sums_scratch(len(chunks), k, rows, low, high),
        compiler_params=pltpu.CompilerParams(vmem_limit_bytes=8 << 20),
        name="early_sums",
    )(ends, *chunks)


def score_kernel(offsets, low, n_blocks, ends_ref, scale_ref, select_ref, labels_ref, early_ref, *refs):
    n_chunks = len(offsets)
    chunks, held = refs[:n_chunks], refs[n_chunks : n_chunks + 2]
    near_ref, far_ref, acts, left, right, outer, sketch = refs[n_chunks + 2 :]
    k = chunks[0].shape[0] // 2
    me, lanes = lax.axis_index("dp"), outer.shape[2]
    sums = outer_sums(offsets, low, ends_ref, chunks, acts, left, right) + early_ref[...]
    for m in range(outer.shape[0]):
        outer[m] = sums[:, m * lanes : (m + 1) * lanes]

    first = lax.broadcasted_iota(jnp.int32, (low, lanes), 1) < k
    per_block = k // n_blocks
    for block in range(n_blocks):
        apart = me ^ block
        base = pl.multiple_of((apart // 2 + apart % 2 * (n_blocks // 2)) * (per_block * k), lanes)
        for i in range(block * per_block, (block + 1) * per_block, 2):
            at = pl.ds(base + (i - block * per_block) * k, lanes)
            for m in range(outer.shape[0]):
                scale = scale_ref[:, m * lanes : (m + 1) * lanes]
                even = outer[m, i * low : (i + 1) * low, :] * scale
                odd = outer[m, (i + 1) * low : (i + 2) * low, :] * scale
                pair = [
                    jnp.where(first, even, pltpu.roll(odd, k, 1)),
                    jnp.where(first, pltpu.roll(even, k, 1), odd),
                ]
                rows_at = slice(2 * m * low, 2 * (m + 1) * low)
                sketch[rows_at, at] = jnp.concatenate(pair, axis=0).astype(BF16)

    half = held[0].shape[1]
    local = sum(
        lax.dot_general(
            ref[...], sketch[:, h * half : (h + 1) * half], NT, preferred_element_type=F32
        )
        for h, ref in enumerate(held)
    )
    packed = lax.dot_general(
        select_ref[...], local.astype(BF16), NT, preferred_element_type=F32
    )
    packed = (packed + labels_ref[...]).astype(BF16)
    near_ref[...], far_ref[...] = packed[: near_ref.shape[0]], packed[near_ref.shape[0] :]


def score(offsets, ends, scale, select, labels, early, chunks, held, nval, low, n_blocks):
    k, rows = chunks[0].shape[0] // 2, chunks[0].shape[1]
    docs = ends.shape[0]
    high = docs // low
    vmem = pl.BlockSpec(memory_space=pltpu.VMEM)
    return pl.pallas_call(
        functools.partial(score_kernel, offsets, low, n_blocks),
        out_shape=[jax.ShapeDtypeStruct((select.shape[0] // 2, nval), BF16)] * 2,
        in_specs=[vmem] * (5 + len(chunks) + 2),
        out_specs=[vmem] * 2,
        scratch_shapes=sums_scratch(len(chunks), k, rows, low, high)
        + [pltpu.VMEM((high // 2, low * k, 2 * k), F32), pltpu.VMEM((docs, k * k), BF16)],
        compiler_params=pltpu.CompilerParams(vmem_limit_bytes=16 << 20),
        cost_estimate=pl.CostEstimate(
            flops=2 * k * k * docs * (len(chunks) * rows + nval),
            bytes_accessed=2 * k * k * nval,
            transcendentals=0,
        ),
        name="score",
    )(ends, scale, select, labels, early, *chunks, *held)


def shards(activations, out_grads, proj_in, proj_out, validation, doc_lengths, owner_rows):
    devices, parts = lax.axis_size("dp"), lax.axis_size("tensor")
    maxdoc = doc_lengths.shape[1]

    nval = validation.shape[0]
    held = validation
    bits = [1 << i for i in range(devices.bit_length() - 1)]
    for bit in bits[1:]:
        held = jnp.concatenate([held, swap(held, "dp", bit)], axis=1)
    halves = (held, swap(held, "dp", bits[0]))

    wa, wg = proj_in.T, proj_out.T
    peers = list(range(parts - 1, 0, -1))
    sent, *kept = project_peers(parts, activations, out_grads, wa, wg)
    got = [swap(sent[i], "tensor", peer) for i, peer in enumerate(peers)]
    total = project_own(activations, *kept, 2).astype(F32)
    for piece in got:
        total = total + piece.astype(F32)
    summed = total.astype(BF16)
    summed, lengths, out_rows = lax.optimization_barrier((summed, doc_lengths[0], owner_rows[0]))
    chunks = [summed] + [swap(summed, "tensor", peer) for peer in range(1, parts)]

    indices = jnp.arange(maxdoc, dtype=jnp.int32)
    starts = jnp.sum(jnp.where(indices[:, None] < indices[None, :], lengths[:, None], 0), axis=0)
    low = maxdoc // 4
    ends = jnp.broadcast_to((starts + lengths)[:, None], (maxdoc, 128))
    scaling = 1.0 / jnp.sqrt(jnp.maximum(lengths, 1).astype(F32))
    scale = jnp.repeat(scaling.reshape(4, low).T, proj_in.shape[1], axis=1)

    per_owner = max(1, maxdoc // devices)
    height = -(-2 * per_owner // 8) * 8
    owners, out_slot = out_rows // maxdoc, out_rows % maxdoc
    earlier = (owners[None, :] == owners[:, None]) & (indices[None, :] < indices[:, None])
    within = jnp.sum(earlier.astype(jnp.int32), axis=1)
    apart = owners ^ lax.axis_index("dp")
    target = (apart // 2 + apart % 2 * (devices // 2)) * height + within
    at = jnp.arange(devices * height, dtype=jnp.int32)
    select = (target[None, :] == at[:, None]).astype(BF16)
    label = jnp.where(lengths > 0, out_slot, -1)
    labels = jnp.sum(
        jnp.where(target[None, :] + per_owner == at[:, None], label[None, :], 0), axis=1
    )
    labels = jnp.broadcast_to(labels.astype(F32)[:, None], (devices * height, nval))

    soon = [0, 2]
    late = [c for c in range(parts) if c not in soon]
    early = early_sums(soon, ends, [chunks[c] for c in soon], low)
    near, away = score(
        late, ends, scale, select, labels, early, [chunks[c] for c in late], halves, nval, low, devices
    )
    crossed = swap(away, "dp", 1)
    blocks = [slice(i * height, (i + 1) * height) for i in range(devices // 2)]
    rows = [jnp.concatenate([near[at], crossed[at]], axis=0) for at in blocks]
    rows = rows[:1] + [swap(rows[i], "dp", 2 * i) for i in range(1, devices // 2)]
    got_rows = jnp.concatenate(rows, axis=0).reshape(devices, height, nval)
    data = got_rows[:, :per_owner].reshape(devices * per_owner, nval)
    tags = got_rows[:, per_owner : 2 * per_owner, :maxdoc].reshape(devices * per_owner, maxdoc)
    choose = (tags.astype(F32) == indices.astype(F32)[None, :]).astype(BF16)
    return lax.dot_general(
        choose, data, (((0,), (0,)), ((), ())), preferred_element_type=F32
    ).astype(BF16)


def solution(mesh):
    placed = (
        P("dp", "tensor"),
        P("dp", "tensor"),
        P("tensor", None),
        P("tensor", None),
        P("tensor", "dp"),
        P("dp", None),
        P("dp", None),
    )
    return jax.shard_map(
        shards, mesh=mesh, in_specs=placed, out_specs=P("dp", "tensor"), check_vma=False
    )
```

```python
import functools

import jax
import jax.numpy as jnp
from jax import lax
from jax.experimental import pallas as pl
from jax.experimental.pallas import tpu as pltpu
from jax.sharding import PartitionSpec as P


BF16, F32 = jnp.bfloat16, jnp.float32
NT = (((1,), (1,)), ((), ()))
VMEM_LIMIT = 24 << 20


def far(x):
    return pltpu.with_memory_space_constraint(x, pltpu.HBM)


def swap(x, axis, k):
    return lax.ppermute(x, axis, [(i, i ^ k) for i in range(lax.axis_size(axis))])


def both_projections(act, grad, wa, wg):
    left = lax.dot_general(act, wa, NT, preferred_element_type=F32)
    right = lax.dot_general(grad, wg, NT, preferred_element_type=F32)
    return jnp.concatenate([left, right], axis=1).T.astype(BF16)


def peers_kernel(
    ahead, act_hbm, grad_hbm, wa_hbm, wg_hbm, *refs
):
    *outs, grad_own, wa, wg, act, grad, sem, wsem = refs
    count, rows = act.shape[0], act.shape[1]
    part = lax.axis_index("tensor")

    def rows_of(chunk):
        return pl.ds(pl.multiple_of(chunk * rows, rows), rows)

    def act_copies(at, i):
        wide = act.shape[2] // 2
        return [
            pltpu.make_async_copy(
                act_hbm.at[at, pl.ds(j * wide, wide)], act.at[i, :, pl.ds(j * wide, wide)], sem.at[1 + j, i]
            )
            for j in range(2)
        ]

    def copies(i):
        at = rows_of(part ^ (count - i))
        return (
            pltpu.make_async_copy(grad_hbm.at[at], grad.at[i], sem.at[0, i]),
            *act_copies(at, i),
        )

    weights = (
        pltpu.make_async_copy(wg_hbm, wg, wsem.at[0]),
        pltpu.make_async_copy(wa_hbm, wa, wsem.at[1]),
    )
    own = pltpu.make_async_copy(grad_hbm.at[rows_of(part)], grad_own, wsem.at[2])
    for copy in weights:
        copy.start()
    for copy in copies(0):
        copy.start()
    for copy in weights:
        copy.wait()
    for i in range(1, min(ahead, count)):
        for copy in copies(i):
            copy.start()

    def step(i, carry):
        for copy in copies(i):
            copy.wait()

        @pl.when(i + ahead < count)
        def _():
            for copy in copies(i + ahead):
                copy.start()

        @pl.when(i + ahead == count)
        def _():
            own.start()

        both = both_projections(act[i], grad[i], wa[...], wg[...])
        for j, ref in enumerate(outs):

            @pl.when(i == j)
            def _(ref=ref):
                ref[...] = both

        return carry

    lax.fori_loop(0, count, step, 0)
    own.wait()


def project_peers(parts, activations, out_grads, wa, wg):
    (tokens, ff), d, k = activations.shape, out_grads.shape[1], wa.shape[0]
    rows, count = tokens // parts, parts - 1
    hbm, vmem = pl.BlockSpec(memory_space=pl.ANY), pl.BlockSpec(memory_space=pltpu.VMEM)
    return pl.pallas_call(
        functools.partial(peers_kernel, min(3, count)),
        out_shape=[
            jax.ShapeDtypeStruct(shape, BF16)
            for shape in [(2 * k, rows)] * count + [(rows, d), (k, ff), (k, d)]
        ],
        in_specs=[hbm] * 4,
        out_specs=[vmem] * (count + 3),
        scratch_shapes=[
            pltpu.VMEM((count, rows, ff), BF16),
            pltpu.VMEM((count, rows, d), BF16),
            pltpu.SemaphoreType.DMA((3, count)),
            pltpu.SemaphoreType.DMA((3,)),
        ],
        compiler_params=pltpu.CompilerParams(vmem_limit_bytes=VMEM_LIMIT),
        cost_estimate=pl.CostEstimate(
            flops=2 * tokens * (ff + d) * k, bytes_accessed=2 * tokens * (ff + d), transcendentals=0
        ),
        name="project_peers",
    )(far(activations), far(out_grads), far(wa), far(wg))


def own_kernel(act_hbm, grad_ref, wa_ref, wg_ref, out_ref, act, sem):
    blocks, rows = act.shape[0], act.shape[1]
    part = lax.axis_index("tensor")

    def copy(i):
        start = pl.multiple_of((part * blocks + i) * rows, rows)
        return pltpu.make_async_copy(act_hbm.at[pl.ds(start, rows)], act.at[i], sem.at[i])

    for i in range(blocks):
        copy(i).start()

    def step(i, carry):
        copy(i).wait()
        at = pl.ds(pl.multiple_of(i * rows, rows), rows)
        out_ref[:, at] = both_projections(act[i], grad_ref[at, :], wa_ref[...], wg_ref[...])
        return carry

    lax.fori_loop(0, blocks, step, 0)


def project_own(activations, grad, wa, wg, blocks):
    hbm, vmem = pl.BlockSpec(memory_space=pl.ANY), pl.BlockSpec(memory_space=pltpu.VMEM)
    ff, (rows, d), k = activations.shape[1], grad.shape, wa.shape[0]
    return pl.pallas_call(
        own_kernel,
        out_shape=jax.ShapeDtypeStruct((2 * k, rows), BF16),
        in_specs=[hbm] + [vmem] * 3,
        out_specs=vmem,
        scratch_shapes=[
            pltpu.VMEM((blocks, rows // blocks, ff), BF16),
            pltpu.SemaphoreType.DMA((blocks,)),
        ],
        compiler_params=pltpu.CompilerParams(vmem_limit_bytes=VMEM_LIMIT),
        cost_estimate=pl.CostEstimate(
            flops=2 * rows * (ff + d) * k, bytes_accessed=2 * rows * (ff + d), transcendentals=0
        ),
        name="project_own",
    )(far(activations), grad, wa, wg)


def outer_sums(offsets, low, ends_ref, chunks, acts, left, right):
    k, rows = chunks[0].shape[0] // 2, chunks[0].shape[1]
    docs, high = ends_ref.shape[0], right.shape[0] // k
    part = lax.axis_index("tensor")
    for c, ref in enumerate(chunks):
        at = (part ^ offsets[c]) * rows + lax.broadcasted_iota(jnp.int32, (docs, rows), 1)
        doc = jnp.sum((at >= ends_ref[:, :1]).astype(F32), axis=0, keepdims=True)
        div = jnp.floor(doc * (1.0 / low))
        of_mod = lax.broadcasted_iota(jnp.int32, (low, rows), 0).astype(F32)
        mod = (jnp.broadcast_to(doc - div * low, (low, rows)) == of_mod).astype(F32)
        span = slice(c * rows, (c + 1) * rows)
        acts[...] = ref[:k, :].astype(F32)
        for i in range(0, k, 2):
            pair = [jnp.broadcast_to(acts[j : j + 1, :], (low, rows)) * mod for j in (i, i + 1)]
            left[i * low : (i + 2) * low, span] = jnp.concatenate(pair, axis=0).astype(BF16)
        for m in range(high):
            mask = jnp.broadcast_to((div == m).astype(F32), (k, rows)).astype(BF16)
            right[m * k : (m + 1) * k, span] = ref[k:, :] * mask
    return lax.dot_general(left[...], right[...], NT, preferred_element_type=F32)


def sums_scratch(count, k, rows, low, high):
    return [
        pltpu.VMEM((k, rows), F32),
        pltpu.VMEM((low * k, count * rows), BF16),
        pltpu.VMEM((high * k, count * rows), BF16),
    ]


def early_kernel(offsets, low, ends_ref, *refs):
    *chunks, out_ref, acts, left, right = refs
    out_ref[...] = outer_sums(offsets, low, ends_ref, chunks, acts, left, right)


def early_sums(offsets, ends, chunks, low):
    vmem = pl.BlockSpec(memory_space=pltpu.VMEM)
    k, rows = chunks[0].shape[0] // 2, chunks[0].shape[1]
    high = ends.shape[0] // low
    return pl.pallas_call(
        functools.partial(early_kernel, offsets, low),
        out_shape=jax.ShapeDtypeStruct((low * k, high * k), F32),
        in_specs=[vmem] * (1 + len(chunks)),
        out_specs=vmem,
        scratch_shapes=sums_scratch(len(chunks), k, rows, low, high),
        compiler_params=pltpu.CompilerParams(vmem_limit_bytes=8 << 20),
        name="early_sums",
    )(ends, *chunks)


def score_kernel(offsets, low, n_blocks, ends_ref, scale_ref, select_ref, labels_ref, early_ref, *refs):
    n_chunks = len(offsets)
    chunks, held = refs[:n_chunks], refs[n_chunks : n_chunks + 2]
    near_ref, far_ref, acts, left, right, outer, sketch = refs[n_chunks + 2 :]
    k = chunks[0].shape[0] // 2
    me, lanes = lax.axis_index("dp"), outer.shape[2]
    sums = outer_sums(offsets, low, ends_ref, chunks, acts, left, right) + early_ref[...]
    for m in range(outer.shape[0]):
        outer[m] = sums[:, m * lanes : (m + 1) * lanes]

    first = lax.broadcasted_iota(jnp.int32, (low, lanes), 1) < k
    per_block = k // n_blocks
    for block in range(n_blocks):
        apart = me ^ block
        base = pl.multiple_of((apart // 2 + apart % 2 * (n_blocks // 2)) * (per_block * k), lanes)
        for i in range(block * per_block, (block + 1) * per_block, 2):
            at = pl.ds(base + (i - block * per_block) * k, lanes)
            for m in range(outer.shape[0]):
                even = outer[m, i * low : (i + 1) * low, :]
                odd = outer[m, (i + 1) * low : (i + 2) * low, :]
                pair = [
                    jnp.where(first, even, pltpu.roll(odd, k, 1)),
                    jnp.where(first, pltpu.roll(even, k, 1), odd),
                ]
                rows_at = slice(2 * m * low, 2 * (m + 1) * low)
                sketch[rows_at, at] = jnp.concatenate(pair, axis=0).astype(BF16)

    half = held[0].shape[1]
    local = sum(
        lax.dot_general(
            ref[...], sketch[:, h * half : (h + 1) * half], NT, preferred_element_type=F32
        )
        for h, ref in enumerate(held)
    )
    packed = lax.dot_general(
        select_ref[...], (local * scale_ref[...]).astype(BF16), NT, preferred_element_type=F32
    )
    packed = (packed + labels_ref[...]).astype(BF16)
    near_ref[...], far_ref[...] = packed[: near_ref.shape[0]], packed[near_ref.shape[0] :]


def score(offsets, ends, scale, select, labels, early, chunks, held, nval, low, n_blocks):
    k, rows = chunks[0].shape[0] // 2, chunks[0].shape[1]
    docs = ends.shape[0]
    high = docs // low
    vmem = pl.BlockSpec(memory_space=pltpu.VMEM)
    return pl.pallas_call(
        functools.partial(score_kernel, offsets, low, n_blocks),
        out_shape=[jax.ShapeDtypeStruct((select.shape[0] // 2, nval), BF16)] * 2,
        in_specs=[vmem] * (5 + len(chunks) + 2),
        out_specs=[vmem] * 2,
        scratch_shapes=sums_scratch(len(chunks), k, rows, low, high)
        + [pltpu.VMEM((high // 2, low * k, 2 * k), F32), pltpu.VMEM((docs, k * k), BF16)],
        compiler_params=pltpu.CompilerParams(vmem_limit_bytes=16 << 20),
        cost_estimate=pl.CostEstimate(
            flops=2 * k * k * docs * (len(chunks) * rows + nval),
            bytes_accessed=2 * k * k * nval,
            transcendentals=0,
        ),
        name="score",
    )(ends, scale, select, labels, early, *chunks, *held)


def shards(activations, out_grads, proj_in, proj_out, validation, doc_lengths, owner_rows):
    devices, parts = lax.axis_size("dp"), lax.axis_size("tensor")
    maxdoc = doc_lengths.shape[1]

    nval = validation.shape[0]
    held = validation
    bits = [1 << i for i in range(devices.bit_length() - 1)]
    for bit in bits[1:]:
        held = jnp.concatenate([held, swap(held, "dp", bit)], axis=1)
    halves = (held, swap(held, "dp", bits[0]))

    wa, wg = proj_in.T, proj_out.T
    peers = list(range(parts - 1, 0, -1))
    made = project_peers(parts, activations, out_grads, wa, wg)
    sent, kept = made[: parts - 1], made[parts - 1 :]
    got = [swap(sent[i], "tensor", peer) for i, peer in enumerate(peers)]
    total = project_own(activations, *kept, 2).astype(F32)
    for piece in got:
        total = total + piece.astype(F32)
    summed = total.astype(BF16)
    summed, lengths, out_rows = lax.optimization_barrier((summed, doc_lengths[0], owner_rows[0]))
    chunks = [summed] + [swap(summed, "tensor", peer) for peer in range(1, parts)]

    indices = jnp.arange(maxdoc, dtype=jnp.int32)
    starts = jnp.sum(jnp.where(indices[:, None] < indices[None, :], lengths[:, None], 0), axis=0)
    low = maxdoc // 4
    ends = jnp.broadcast_to((starts + lengths)[:, None], (maxdoc, 128))
    scale = (1.0 / jnp.sqrt(jnp.maximum(lengths, 1).astype(F32)))[None, :]

    per_owner = max(1, maxdoc // devices)
    height = -(-2 * per_owner // 8) * 8
    owners, out_slot = out_rows // maxdoc, out_rows % maxdoc
    earlier = (owners[None, :] == owners[:, None]) & (indices[None, :] < indices[:, None])
    within = jnp.sum(earlier.astype(jnp.int32), axis=1)
    apart = owners ^ lax.axis_index("dp")
    target = (apart // 2 + apart % 2 * (devices // 2)) * height + within
    at = jnp.arange(devices * height, dtype=jnp.int32)
    select = (target[None, :] == at[:, None]).astype(BF16)
    label = jnp.where(lengths > 0, out_slot, -1)
    labels = jnp.sum(
        jnp.where(target[None, :] + per_owner == at[:, None], label[None, :], 0), axis=1
    )
    labels = jnp.broadcast_to(labels.astype(F32)[:, None], (devices * height, nval))

    soon = [0, 2]
    late = [c for c in range(parts) if c not in soon]
    early = early_sums(soon, ends, [chunks[c] for c in soon], low)
    near, away = score(
        late, ends, scale, select, labels, early, [chunks[c] for c in late], halves, nval, low, devices
    )
    crossed = swap(away, "dp", 1)
    blocks = [slice(i * height, (i + 1) * height) for i in range(devices // 2)]
    rows = [jnp.concatenate([near[at], crossed[at]], axis=0) for at in blocks]
    rows = rows[:1] + [swap(rows[i], "dp", 2 * i) for i in range(1, devices // 2)]
    got_rows = jnp.concatenate(rows, axis=0).reshape(devices, height, nval)
    data = got_rows[:, :per_owner].reshape(devices * per_owner, nval)
    tags = got_rows[:, per_owner : 2 * per_owner, :maxdoc].reshape(devices * per_owner, maxdoc)
    choose = (tags.astype(F32) == indices.astype(F32)[None, :]).astype(BF16)
    return lax.dot_general(
        choose, data, (((0,), (0,)), ((), ())), preferred_element_type=F32
    ).astype(BF16)


def solution(mesh):
    placed = (
        P("dp", "tensor"),
        P("dp", "tensor"),
        P("tensor", None),
        P("tensor", None),
        P("tensor", "dp"),
        P("dp", None),
        P("dp", None),
    )
    return jax.shard_map(
        shards, mesh=mesh, in_specs=placed, out_specs=P("dp", "tensor"), check_vma=False
    )
```
